32 devices in a mesh: wide: 16 (over z, y, x), narrow: 2 (over core).
Axes of the slice: x: 2, y: 2, z: 4, core: 2. Of those that a mesh axis runs over, the one named last changes fastest.
Arguments:
- passages: bfloat16 [16384, 768], P('wide'), may hold values from -32 to 32
- centroids: bfloat16 [4096, 768], P('narrow'), may hold values from -6 to 6
Outputs:
- new_centroids: float32 [4096, 768], P('narrow')
- row_potential: float32 [16384], P('wide')
- col_potential: float32 [4096], P('narrow')
The draws below stay inside these ranges and needn't reach their ends.
All inputs are finite; a program needn't handle non-finite values.
Results may differ from the reference program's by a relative error of at most 0.00035.
Values sent between devices are 32-bit elements; how exact they have to be, the bound alone decides.
A program may use at most 64 MiB of HBM per device.

```python
import math
import jax
import jax.numpy as jnp
from jax import lax

VECTOR_DIMENSION = 768
CENTROIDS = 4096
SWEEPS = 3
PASSAGE_TOTAL = 16384


def draw_passages(key, part):
    noise_key = jax.random.fold_in(key, 11)
    mean_key = jax.random.fold_in(key, 23)
    shared = jax.random.truncated_normal(mean_key, -4.0, 4.0, (1, VECTOR_DIMENSION), jnp.float32)
    noise = jax.random.truncated_normal(noise_key, -6.0, 6.0, (PASSAGE_TOTAL, VECTOR_DIMENSION), jnp.float32)
    return (noise + 0.3 * shared).astype(jnp.bfloat16)


def levels(rng, shape, cuts, smallest, high):
    def one(position, blocks):
        steps = jax.random.uniform(jax.random.fold_in(jax.random.fold_in(rng, 6), position), (blocks,), jnp.float32, smallest / len(cuts), high / len(cuts))
        return jnp.repeat(jnp.exp(steps), shape[position] // blocks).reshape((-1,) + (1,) * (len(shape) - position - 1))

    gain = one(*cuts[0])
    for cut in cuts[1:]:
        gain = gain * one(*cut)
    return gain


def gaussian(stream_key, shape, scale, limit, split=(), dtype=jnp.bfloat16):
    factor_of = levels(stream_key, shape, split, -0.22, 0.18) if split else 1.0
    drawn = jax.random.normal(stream_key, shape, jnp.float32) * scale * factor_of
    return jnp.minimum(jnp.maximum(drawn, -limit), limit).astype(dtype)


def setup_inputs(seed: int = 0) -> dict:
    splits = jax.random.split(jax.random.key(seed), 3)
    passages = draw_passages(jax.random.fold_in(splits[2], 71), 0)
    centroids = gaussian(splits[1], (CENTROIDS, VECTOR_DIMENSION), 1.0, 6.0, ((0, 2),))
    return {"passages": passages, "centroids": centroids}


entropic_regularizer = 0.02

def inverse_rms(values):
    wide_values = values.astype(jnp.float32)
    return lax.rsqrt(lax.optimization_barrier(jnp.mean(wide_values * wide_values, axis=1)) + 1e-06)

def kernel_block(rows, normalized_vectors, centroids, cluster_center_factor):
    cosine_affinity_matrix = jnp.dot(rows, centroids.T, preferred_element_type=jnp.float32)
    return jnp.exp(cosine_affinity_matrix * normalized_vectors[:, None] * cluster_center_factor[None, :] * (1.0 / (VECTOR_DIMENSION * entropic_regularizer)))

def reference(passages, centroids):
    width = math.gcd(PASSAGE_TOTAL, 4096)
    count = PASSAGE_TOTAL // width
    passage_row_scale = inverse_rms(passages)
    cluster_center_factor = inverse_rms(centroids)
    grouped = passages.reshape(count, width, VECTOR_DIMENSION)
    cluster_gathered_factor = passage_row_scale.reshape(count, width)
    target = PASSAGE_TOTAL / CENTROIDS

    def balance(col_factor):

        def advance(column_mass, item):
            rows, normalized_vectors = item
            kernel = kernel_block(rows, normalized_vectors, centroids, cluster_center_factor)
            row_factor = 1.0 / jnp.dot(kernel, col_factor, precision=lax.Precision.HIGHEST)
            column_mass = column_mass + jnp.dot(row_factor, kernel, precision=lax.Precision.HIGHEST)
            return (column_mass, row_factor)
        column_mass, row_factor = lax.scan(advance, jnp.zeros((CENTROIDS,), jnp.float32), (grouped, cluster_gathered_factor))
        return (target / column_mass, row_factor)
    col_factor = jnp.ones((CENTROIDS,), jnp.float32)
    row_factor = jnp.ones((count, width), jnp.float32)
    for number in range(SWEEPS):
        col_factor, row_factor = balance(col_factor)

    def accumulate(totals, item):
        rows, normalized_vectors, factors = item
        kernel = kernel_block(rows, normalized_vectors, centroids, cluster_center_factor)
        weights = (factors[:, None] * kernel * col_factor[None, :] * normalized_vectors[:, None]).astype(jnp.bfloat16)
        return (totals + jnp.dot(weights.T, rows, preferred_element_type=jnp.float32), None)
    totals, discarded_output = lax.scan(accumulate, jnp.zeros((CENTROIDS, VECTOR_DIMENSION), jnp.float32), (grouped, cluster_gathered_factor, row_factor))
    new_centroids = totals * lax.rsqrt(lax.optimization_barrier(jnp.mean(totals * totals, axis=1, keepdims=True)) + 1e-06)
    row_potential = jnp.log(CENTROIDS * row_factor.reshape(PASSAGE_TOTAL))
    return (new_centroids, row_potential, jnp.log(col_factor))
```

```python
import functools

import jax
import jax.numpy as jnp
from jax import lax
from jax.experimental import pallas as pl
from jax.experimental.pallas import tpu as pltpu
from jax.sharding import PartitionSpec as P

VECTOR_DIMENSION = 768
CENTROIDS = 4096
SWEEPS = 3
LANES = 128
CHUNKS = 4
MESH = pl.DeviceIdType.MESH

entropic_regularizer = 0.02
LOG2_E = 1.4426950408889634


def unit_rows(totals):
    return totals * lax.rsqrt(jnp.mean(totals * totals, axis=1, keepdims=True) + 1e-06)


def lane_groups(values):
    total = values[:, :LANES]
    for start in range(LANES, values.shape[1], LANES):
        total = total + values[:, start : start + LANES]
    return total


def to_lanes(values):
    ones = jnp.ones((8, LANES), jnp.float32)
    sums = lax.dot_general(
        ones, values, (((1,), (1,)), ((), ())),
        precision=lax.Precision.HIGHEST, preferred_element_type=jnp.float32,
    )
    return sums[0:1, :]


def kernel(
    n_wide, n_narrow, reduce_here,
    p_ref, c_ref, out_ref, rowpot_ref, colpot_ref,
    k_ref, scale_ref, cent_ref, col_ref, row_ref,
    rows_ref, mass_ref, rows_send, rows_recv, mass_send, mass_recv, *reduce_refs,
):
    m, n = k_ref.shape
    wide, narrow = lax.axis_index("wide"), lax.axis_index("narrow")

    barrier = pltpu.get_barrier_semaphore()

    def greet_wide(step, carry):
        pl.semaphore_signal(
            barrier, inc=1, device_id={"wide": lax.rem(wide + step, n_wide)}, device_id_type=MESH
        )
        return carry

    def greet_narrow(step, carry):
        pl.semaphore_signal(
            barrier, inc=1, device_id={"narrow": lax.rem(narrow + step, n_narrow)}, device_id_type=MESH
        )
        return carry

    lax.fori_loop(1, n_wide, greet_wide, 0)
    lax.fori_loop(1, n_narrow, greet_narrow, 0)

    cb = 256
    for j in range(n // cb):
        values = c_ref[j * cb : (j + 1) * cb, :].astype(jnp.float32)
        squares = to_lanes(lane_groups(values * values))
        cent_ref[:, j * cb : (j + 1) * cb] = lax.rsqrt(
            squares * (1.0 / VECTOR_DIMENSION) + 1e-06
        ) * (LOG2_E / (VECTOR_DIMENSION * entropic_regularizer))

    bm, bn = 256, 512

    @pl.loop(0, m // bm)
    def _(i):
        at = pl.ds(pl.multiple_of(i * bm, bm), bm)
        block = p_ref[at, :]
        values = block.astype(jnp.float32)
        scale = lax.rsqrt(
            jnp.sum(lane_groups(values * values), axis=1, keepdims=True) * (1.0 / VECTOR_DIMENSION) + 1e-06
        )
        scale_ref[at, :] = jnp.broadcast_to(scale, (bm, LANES))
        total = jnp.zeros((bm, LANES), jnp.float32)
        for j in range(n // bn):
            cols = slice(j * bn, (j + 1) * bn)
            scores = lax.dot_general(
                block, c_ref[cols, :], (((1,), (1,)), ((), ())), preferred_element_type=jnp.float32
            )
            entries = jnp.exp2(scores * scale * cent_ref[:, cols])
            k_ref[at, cols] = entries
            total = total + lane_groups(entries)
        rows_ref[0, pl.ds(narrow, 1), :, at] = to_lanes(total)[None]

    pl.semaphore_wait(barrier, n_wide - 1 + n_narrow - 1)

    target = float(n_wide * m) / float(n_narrow * n)
    rb = 128

    def exchange(sweep, buffer, axis, me, size, send, recv):
        def copy(peer, slot):
            return pltpu.make_async_remote_copy(
                src_ref=buffer.at[sweep, slot],
                dst_ref=buffer.at[sweep, slot],
                send_sem=send.at[sweep, peer],
                recv_sem=recv.at[sweep, slot],
                device_id={axis: peer},
                device_id_type=MESH,
            )

        def start(step, carry):
            copy(lax.rem(me + step, size), me).start()
            return carry

        def arrive(step, carry):
            peer = lax.rem(me + step, size)
            copy(peer, peer).wait_recv()
            return carry

        def sent(step, carry):
            copy(lax.rem(me + step, size), me).wait_send()
            return carry

        lax.fori_loop(1, size, start, 0)
        lax.fori_loop(1, size, arrive, 0)
        lax.fori_loop(1, size, sent, 0)
        total = buffer[sweep, 0]
        for slot in range(1, size):
            total = total + buffer[sweep, slot]
        return total

    for sweep in range(SWEEPS):
        if sweep > 0:

            @pl.loop(0, m // rb)
            def _(i):
                at = pl.ds(pl.multiple_of(i * rb, rb), rb)
                total = jnp.zeros((rb, LANES), jnp.float32)
                for t in range(n // LANES):
                    cols = slice(t * LANES, (t + 1) * LANES)
                    total = total + k_ref[at, cols] * col_ref[:, cols]
                rows_ref[sweep, pl.ds(narrow, 1), :, at] = to_lanes(total)[None]

        row_factor = 1.0 / exchange(sweep, rows_ref, "narrow", narrow, n_narrow, rows_send, rows_recv)
        row_ref[...] = row_factor

        last = sweep == SWEEPS - 1

        def mass_step(i, partial):
            at = pl.ds(pl.multiple_of(i * rb, rb), rb)
            factor = jnp.transpose(jnp.broadcast_to(row_ref[:, at], (LANES, rb)))
            if last:
                scale_ref[at, :] = scale_ref[at, :] * factor
            sums = []
            for t in range(n // LANES):
                cols = slice(t * LANES, (t + 1) * LANES)
                product = k_ref[at, cols] * factor
                sums.append(partial[t] + jnp.sum(product.reshape(rb // 8, 8, LANES), axis=0))
            return tuple(sums)

        zeros = tuple(jnp.zeros((8, LANES), jnp.float32) for _ in range(n // LANES))
        sums = lax.fori_loop(0, m // rb, mass_step, zeros)
        for t in range(n // LANES):
            mass_ref[sweep, pl.ds(wide, 1), :, t * LANES : (t + 1) * LANES] = jnp.sum(
                sums[t], axis=0, keepdims=True
            )[None]
        if last:
            rowpot_ref[...] = jnp.log(CENTROIDS * row_factor)
        col_ref[...] = target / exchange(sweep, mass_ref, "wide", wide, n_wide, mass_send, mass_recv)

    colpot_ref[...] = jnp.log(col_ref[...])

    tb = 128

    def totals_block(into, start):
        cols = pl.ds(pl.multiple_of(start, tb), tb)
        weights = (k_ref[:, cols] * scale_ref[...] * col_ref[:, cols]).astype(jnp.bfloat16)
        into[cols, :] = lax.dot_general(
            weights, p_ref[...], (((0,), (0,)), ((), ())), preferred_element_type=jnp.float32
        )

    if not reduce_here:

        @pl.loop(0, n // tb)
        def _(j):
            totals_block(out_ref, j * tb)

        return

    t_ref, got1, got2, got3, s1, r1, s2, r2, s3, r3, s4, r4, s5, r5, s6, r6 = reduce_refs
    line = n_wide // 4
    half = n // 2
    r = half // CHUNKS
    z, y, x = wide // 4, lax.rem(wide // 2, 2), lax.rem(wide, 2)
    over_x = z * 4 + y * 2 + (1 - x)
    over_y = z * 4 + (1 - y) * 2 + x
    partners = ((over_x, over_y), (over_y, over_x))
    bits = ((x, y), (y, x))
    plane = lax.rem(wide, 4)

    def rows_of(start, size):
        return pl.ds(pl.multiple_of(start, 8), size)

    def remote(src, dst, send, recv, peer):
        return pltpu.make_async_remote_copy(
            src_ref=src, dst_ref=dst, send_sem=send, recv_sem=recv,
            device_id={"wide": peer}, device_id_type=MESH,
        )

    def base(h, k):
        return h * half + k * r

    def my_half(h, k):
        return base(h, k) + bits[h][0] * (r // 2)

    def other_half(h, k):
        return base(h, k) + (1 - bits[h][0]) * (r // 2)

    def my_quarter(h, k):
        return my_half(h, k) + bits[h][1] * (r // 4)

    def other_quarter(h, k):
        return my_half(h, k) + (1 - bits[h][1]) * (r // 4)

    shard = r // 4 // line

    def first(h, k):
        return remote(
            t_ref.at[rows_of(other_half(h, k), r // 2)], got1.at[h, k],
            s1.at[h, k], r1.at[h, k], partners[h][0],
        )

    def second(h, k):
        return remote(
            t_ref.at[rows_of(other_quarter(h, k), r // 4)], got2.at[h, k],
            s2.at[h, k], r2.at[h, k], partners[h][1],
        )

    def third(h, k, peer, slot):
        return remote(
            t_ref.at[rows_of(my_quarter(h, k) + peer * shard, shard)], got3.at[h, k, slot],
            s3.at[h, k, peer], r3.at[h, k, slot], peer * 4 + plane,
        )

    def fourth(h, k, peer, slot):
        piece = rows_of(my_quarter(h, k) + slot * shard, shard)
        return remote(
            out_ref.at[piece], out_ref.at[piece],
            s4.at[h, k, peer], r4.at[h, k, slot], peer * 4 + plane,
        )

    def fifth(h, k, start):
        piece = rows_of(start, r // 4)
        return remote(
            out_ref.at[piece], out_ref.at[piece], s5.at[h, k], r5.at[h, k], partners[h][1]
        )

    def sixth(h, k, start):
        piece = rows_of(start, r // 2)
        return remote(
            out_ref.at[piece], out_ref.at[piece], s6.at[h, k], r6.at[h, k], partners[h][0]
        )

    def others(action):
        for step in range(1, line):
            action(lax.rem(z + step, line))

    pairs = [(h, k) for k in range(CHUNKS) for h in range(2)]

    for h, k in pairs:

        @pl.loop(0, r // tb)
        def _(j):
            totals_block(t_ref, base(h, k) + j * tb)

        first(h, k).start()

    for h, k in pairs:
        first(h, k).wait_recv()
        for q in range(2):
            sends = other_quarter(h, k) if q == 0 else my_quarter(h, k)
            at = rows_of(sends, r // 4)
            t_ref[at, :] = t_ref[at, :] + got1[h, k, rows_of(sends - my_half(h, k), r // 4), :]
            if q == 0:
                second(h, k).start()

    def after_second(h, k):
        second(h, k).wait_recv()
        at = rows_of(my_quarter(h, k), r // 4)
        t_ref[at, :] = t_ref[at, :] + got2[h, k]
        others(lambda peer: third(h, k, peer, z).start())

    def after_third(h, k):
        others(lambda peer: third(h, k, z, peer).wait_recv())
        at = rows_of(my_quarter(h, k) + z * shard, shard)
        total = t_ref[at, :]
        for step in range(1, line):
            total = total + got3[h, k, lax.rem(z + step, line)]
        out_ref[at, :] = unit_rows(total)
        others(lambda peer: fourth(h, k, peer, z).start())

    def after_fourth(h, k):
        others(lambda peer: fourth(h, k, z, peer).wait_recv())
        fifth(h, k, my_quarter(h, k)).start()

    stages = (after_second, after_third, after_fourth)
    for step in range(len(pairs) + 4):
        for number, stage in enumerate(stages):
            index = step - 2 * number
            if 0 <= index < len(pairs):
                stage(*pairs[index])
    for h, k in pairs:
        fifth(h, k, other_quarter(h, k)).wait_recv()
        sixth(h, k, my_half(h, k)).start()
    for h, k in pairs:
        sixth(h, k, other_half(h, k)).wait_recv()
    for h, k in pairs:
        first(h, k).wait_send()
        second(h, k).wait_send()
        others(lambda peer: third(h, k, peer, z).wait_send())
        others(lambda peer: fourth(h, k, peer, z).wait_send())
        fifth(h, k, my_quarter(h, k)).wait_send()
        sixth(h, k, my_half(h, k)).wait_send()


def solution(mesh):
    n_wide, n_narrow = mesh.shape["wide"], mesh.shape["narrow"]

    def body(passages, centroids):
        m, d = passages.shape
        n = centroids.shape[0]
        reduce_here = n_wide % 4 == 0 and n % (8 * 2 * CHUNKS * n_wide) == 0
        dma = pltpu.SemaphoreType.DMA
        scratch = [
            pltpu.VMEM((m, n), jnp.float32),
            pltpu.VMEM((m, LANES), jnp.float32),
            pltpu.VMEM((1, n), jnp.float32),
            pltpu.VMEM((1, n), jnp.float32),
            pltpu.VMEM((1, m), jnp.float32),
            pltpu.VMEM((SWEEPS, n_narrow, 1, m), jnp.float32),
            pltpu.VMEM((SWEEPS, n_wide, 1, n), jnp.float32),
            dma((SWEEPS, n_narrow)),
            dma((SWEEPS, n_narrow)),
            dma((SWEEPS, n_wide)),
            dma((SWEEPS, n_wide)),
        ]
        if reduce_here:
            r = n // 2 // CHUNKS
            line = n_wide // 4
            scratch += [
                pltpu.VMEM((n, d), jnp.float32),
                pltpu.VMEM((2, CHUNKS, r // 2, d), jnp.float32),
                pltpu.VMEM((2, CHUNKS, r // 4, d), jnp.float32),
                pltpu.VMEM((2, CHUNKS, line, r // 4 // line, d), jnp.float32),
            ]
            pair, lines = dma((2, CHUNKS)), dma((2, CHUNKS, line))
            scratch += [pair] * 4 + [lines] * 4 + [pair] * 4
        vmem = pl.BlockSpec(memory_space=pltpu.VMEM)
        totals, row_potential, col_potential = pl.pallas_call(
            functools.partial(kernel, n_wide, n_narrow, reduce_here),
            out_shape=(
                jax.ShapeDtypeStruct((n, d), jnp.float32),
                jax.ShapeDtypeStruct((1, m), jnp.float32),
                jax.ShapeDtypeStruct((1, n), jnp.float32),
            ),
            in_specs=[vmem, vmem],
            out_specs=(vmem, vmem, vmem),
            scratch_shapes=scratch,
            compiler_params=pltpu.CompilerParams(collective_id=0, has_side_effects=True),
        )(passages, centroids)
        if not reduce_here:
            totals = unit_rows(lax.psum(totals, "wide"))
        return totals, row_potential.reshape(m), col_potential.reshape(n)

    in_specs = (P("wide", None), P("narrow", None))
    out_specs = (P("narrow", None), P("wide"), P("narrow"))
    return jax.shard_map(body, mesh=mesh, in_specs=in_specs, out_specs=out_specs, check_vma=False)
```

```python
import functools
import heapq

import jax
import jax.numpy as jnp
from jax import lax
from jax.experimental import pallas as pl
from jax.experimental.pallas import tpu as pltpu
from jax.sharding import PartitionSpec as P

VECTOR_DIMENSION = 768
CENTROIDS = 4096
SWEEPS = 3
LANES = 128
CHUNKS = 8
AHEAD = 2
VMEM_LIMIT = 38 * 1024 * 1024
MESH = pl.DeviceIdType.MESH

entropic_regularizer = 0.02
LOG2_E = 1.4426950408889634


def plan(chunks):
    pairs = [(half, chunk) for chunk in range(chunks) for half in range(2)]
    sizes = (0.5, 0.25, 0.25, 0.25, 0.25, 0.5)
    free = {"x": 0.0, "y": 0.0, "z": 0.0}
    events, order, issued = [], [], 0
    unit = 512.0 / chunks * 0.132

    def send(at, pair, stage):
        axes = ("x", "y") if pair[0] == 0 else ("y", "x")
        link = (axes[0], axes[1], "z", "z", axes[1], axes[0])[stage]
        free[link] = max(at, free[link]) + sizes[stage] * unit
        heapq.heappush(events, (free[link] + (3.4 if link == "z" else 1.8), len(order), pair, stage))

    clock = 0.0
    while issued < min(2 * AHEAD, len(pairs)):
        clock += 3.6 / chunks
        send(clock, pairs[issued], 0)
        issued += 1
    while events:
        at, _, pair, stage = heapq.heappop(events)
        clock = max(clock, at) + (2.8, 1.6, 1.2, 0.1, 0.1, 0.1)[stage] / chunks
        follows = stage == 0 and issued < len(pairs)
        order.append((pair, stage, pairs[issued] if follows else None))
        if stage < 5:
            send(clock, pair, stage + 1)
        if follows:
            clock += 3.6 / chunks
            send(clock, pairs[issued], 0)
            issued += 1
    return order


def unit_rows(totals):
    return totals * lax.rsqrt(jnp.mean(totals * totals, axis=1, keepdims=True) + 1e-06)


def lane_groups(values):
    total = values[:, :LANES]
    for start in range(LANES, values.shape[1], LANES):
        total = total + values[:, start : start + LANES]
    return total


def to_lanes(values):
    ones = jnp.ones((8, LANES), jnp.float32)
    sums = lax.dot_general(
        ones, values, (((1,), (1,)), ((), ())),
        precision=lax.Precision.HIGHEST, preferred_element_type=jnp.float32,
    )
    return sums[0:1, :]


def kernel(
    n_wide, n_narrow, reduce_here,
    p_ref, c_ref, out_ref, rowpot_ref, colpot_ref,
    k_ref, scale_ref, cent_ref, col_ref, row_ref,
    rows_ref, mass_ref, rows_send, rows_recv, mass_send, mass_recv, *reduce_refs,
):
    m, n = k_ref.shape
    wide, narrow = lax.axis_index("wide"), lax.axis_index("narrow")

    barrier = pltpu.get_barrier_semaphore()

    def greet_wide(step, carry):
        pl.semaphore_signal(
            barrier, inc=1, device_id={"wide": lax.rem(wide + step, n_wide)}, device_id_type=MESH
        )
        return carry

    def greet_narrow(step, carry):
        pl.semaphore_signal(
            barrier, inc=1, device_id={"narrow": lax.rem(narrow + step, n_narrow)}, device_id_type=MESH
        )
        return carry

    lax.fori_loop(1, n_wide, greet_wide, 0)
    lax.fori_loop(1, n_narrow, greet_narrow, 0)

    cb = 256
    for j in range(n // cb):
        values = c_ref[j * cb : (j + 1) * cb, :].astype(jnp.float32)
        squares = to_lanes(lane_groups(values * values))
        cent_ref[:, j * cb : (j + 1) * cb] = lax.rsqrt(
            squares * (1.0 / VECTOR_DIMENSION) + 1e-06
        ) * (LOG2_E / (VECTOR_DIMENSION * entropic_regularizer))

    bm, bn = 256, 512

    @pl.loop(0, m // bm)
    def _(i):
        at = pl.ds(pl.multiple_of(i * bm, bm), bm)
        block = p_ref[at, :]
        values = block.astype(jnp.float32)
        scale = lax.rsqrt(
            jnp.sum(lane_groups(values * values), axis=1, keepdims=True) * (1.0 / VECTOR_DIMENSION) + 1e-06
        )
        scale_ref[at, :] = jnp.broadcast_to(scale, (bm, LANES))
        total = jnp.zeros((bm, LANES), jnp.float32)
        for j in range(n // bn):
            cols = slice(j * bn, (j + 1) * bn)
            scores = lax.dot_general(
                block, c_ref[cols, :], (((1,), (1,)), ((), ())), preferred_element_type=jnp.float32
            )
            entries = jnp.exp2(scores * scale * cent_ref[:, cols])
            k_ref[at, cols] = entries
            total = total + lane_groups(entries)
        rows_ref[0, pl.ds(narrow, 1), :, at] = to_lanes(total)[None]

    pl.semaphore_wait(barrier, n_wide - 1 + n_narrow - 1)

    target = float(n_wide * m) / float(n_narrow * n)
    rb = 128

    def exchange(sweep, buffer, axis, me, size, send, recv):
        def copy(peer, slot):
            return pltpu.make_async_remote_copy(
                src_ref=buffer.at[sweep, slot],
                dst_ref=buffer.at[sweep, slot],
                send_sem=send.at[sweep, peer],
                recv_sem=recv.at[sweep, slot],
                device_id={axis: peer},
                device_id_type=MESH,
            )

        def start(step, carry):
            copy(lax.rem(me + step, size), me).start()
            return carry

        def arrive(step, carry):
            peer = lax.rem(me + step, size)
            copy(peer, peer).wait_recv()
            return carry

        def sent(step, carry):
            copy(lax.rem(me + step, size), me).wait_send()
            return carry

        lax.fori_loop(1, size, start, 0)
        lax.fori_loop(1, size, arrive, 0)
        lax.fori_loop(1, size, sent, 0)
        total = buffer[sweep, 0]
        for slot in range(1, size):
            total = total + buffer[sweep, slot]
        return total

    for sweep in range(SWEEPS):
        if sweep > 0:

            @pl.loop(0, m // rb)
            def _(i):
                at = pl.ds(pl.multiple_of(i * rb, rb), rb)
                total = jnp.zeros((rb, LANES), jnp.float32)
                for t in range(n // LANES):
                    cols = slice(t * LANES, (t + 1) * LANES)
                    total = total + k_ref[at, cols] * col_ref[:, cols]
                rows_ref[sweep, pl.ds(narrow, 1), :, at] = to_lanes(total)[None]

        row_factor = 1.0 / exchange(sweep, rows_ref, "narrow", narrow, n_narrow, rows_send, rows_recv)
        row_ref[...] = row_factor

        last = sweep == SWEEPS - 1

        def mass_step(i, partial):
            at = pl.ds(pl.multiple_of(i * rb, rb), rb)
            factor = jnp.transpose(jnp.broadcast_to(row_ref[:, at], (LANES, rb)))
            if last:
                scale_ref[at, :] = scale_ref[at, :] * factor
            sums = []
            for t in range(n // LANES):
                cols = slice(t * LANES, (t + 1) * LANES)
                product = k_ref[at, cols] * factor
                sums.append(partial[t] + jnp.sum(product.reshape(rb // 8, 8, LANES), axis=0))
            return tuple(sums)

        zeros = tuple(jnp.zeros((8, LANES), jnp.float32) for _ in range(n // LANES))
        sums = lax.fori_loop(0, m // rb, mass_step, zeros)
        for t in range(n // LANES):
            mass_ref[sweep, pl.ds(wide, 1), :, t * LANES : (t + 1) * LANES] = jnp.sum(
                sums[t], axis=0, keepdims=True
            )[None]
        if last:
            rowpot_ref[...] = jnp.log(CENTROIDS * row_factor)
        col_ref[...] = target / exchange(sweep, mass_ref, "wide", wide, n_wide, mass_send, mass_recv)

    colpot_ref[...] = jnp.log(col_ref[...])

    tb = 128

    def totals_block(into, start):
        cols = pl.ds(pl.multiple_of(start, tb), tb)
        weights = (k_ref[:, cols] * scale_ref[...] * col_ref[:, cols]).astype(jnp.bfloat16)
        into[cols, :] = lax.dot_general(
            weights, p_ref[...], (((0,), (0,)), ((), ())), preferred_element_type=jnp.float32
        )

    if not reduce_here:

        @pl.loop(0, n // tb)
        def _(j):
            totals_block(out_ref, j * tb)

        return

    t_ref, got1, got2, got3, s1, r1, s2, r2, s3, r3, s4, r4, s5, r5, s6, r6 = reduce_refs
    line = n_wide // 4
    half = n // 2
    r = half // CHUNKS
    z, y, x = wide // 4, lax.rem(wide // 2, 2), lax.rem(wide, 2)
    over_x = z * 4 + y * 2 + (1 - x)
    over_y = z * 4 + (1 - y) * 2 + x
    partners = ((over_x, over_y), (over_y, over_x))
    bits = ((x, y), (y, x))
    plane = lax.rem(wide, 4)

    def rows_of(start, size):
        return pl.ds(pl.multiple_of(start, 8), size)

    def remote(src, dst, send, recv, peer):
        return pltpu.make_async_remote_copy(
            src_ref=src, dst_ref=dst, send_sem=send, recv_sem=recv,
            device_id={"wide": peer}, device_id_type=MESH,
        )

    def base(h, k):
        return h * half + k * r

    def my_half(h, k):
        return base(h, k) + bits[h][0] * (r // 2)

    def other_half(h, k):
        return base(h, k) + (1 - bits[h][0]) * (r // 2)

    def my_quarter(h, k):
        return my_half(h, k) + bits[h][1] * (r // 4)

    def other_quarter(h, k):
        return my_half(h, k) + (1 - bits[h][1]) * (r // 4)

    shard = r // 4 // line

    def first(h, k):
        return remote(
            t_ref.at[rows_of(other_half(h, k), r // 2)], got1.at[h, k],
            s1.at[h, k], r1.at[h, k], partners[h][0],
        )

    def second(h, k):
        return remote(
            t_ref.at[rows_of(other_quarter(h, k), r // 4)], got2.at[h, k],
            s2.at[h, k], r2.at[h, k], partners[h][1],
        )

    def third(h, k, peer, slot):
        return remote(
            t_ref.at[rows_of(my_quarter(h, k) + peer * shard, shard)], got3.at[h, k, slot],
            s3.at[h, k, peer], r3.at[h, k, slot], peer * 4 + plane,
        )

    def fourth(h, k, peer, slot):
        piece = rows_of(my_quarter(h, k) + slot * shard, shard)
        return remote(
            out_ref.at[piece], out_ref.at[piece],
            s4.at[h, k, peer], r4.at[h, k, slot], peer * 4 + plane,
        )

    def fifth(h, k, start):
        piece = rows_of(start, r // 4)
        return remote(
            out_ref.at[piece], out_ref.at[piece], s5.at[h, k], r5.at[h, k], partners[h][1]
        )

    def sixth(h, k, start):
        piece = rows_of(start, r // 2)
        return remote(
            out_ref.at[piece], out_ref.at[piece], s6.at[h, k], r6.at[h, k], partners[h][0]
        )

    def others(action):
        for step in range(1, line):
            action(lax.rem(z + step, line))

    pairs = [(h, k) for k in range(CHUNKS) for h in range(2)]

    def begin(h, k):
        @pl.loop(0, r // tb)
        def _(j):
            totals_block(t_ref, base(h, k) + j * tb)

        first(h, k).start()

    def add_first(h, k, quarter):
        at = rows_of(quarter, r // 4)
        t_ref[at, :] = t_ref[at, :] + got1[h, k, rows_of(quarter - my_half(h, k), r // 4), :]

    def after_first(h, k):
        first(h, k).wait_recv()
        add_first(h, k, other_quarter(h, k))
        second(h, k).start()
        add_first(h, k, my_quarter(h, k))

    def after_second(h, k):
        second(h, k).wait_recv()
        at = rows_of(my_quarter(h, k), r // 4)
        t_ref[at, :] = t_ref[at, :] + got2[h, k]
        others(lambda peer: third(h, k, peer, z).start())

    def after_third(h, k):
        others(lambda peer: third(h, k, z, peer).wait_recv())
        at = rows_of(my_quarter(h, k) + z * shard, shard)
        total = t_ref[at, :]
        for step in range(1, line):
            total = total + got3[h, k, lax.rem(z + step, line)]
        out_ref[at, :] = unit_rows(total)
        others(lambda peer: fourth(h, k, peer, z).start())

    def after_fourth(h, k):
        others(lambda peer: fourth(h, k, z, peer).wait_recv())
        fifth(h, k, my_quarter(h, k)).start()

    def after_fifth(h, k):
        fifth(h, k, other_quarter(h, k)).wait_recv()
        sixth(h, k, my_half(h, k)).start()

    def after_sixth(h, k):
        sixth(h, k, other_half(h, k)).wait_recv()

    stages = (after_first, after_second, after_third, after_fourth, after_fifth, after_sixth)
    for pair in pairs[: 2 * AHEAD]:
        begin(*pair)
    for pair, stage, following in plan(CHUNKS):
        stages[stage](*pair)
        if following is not None:
            begin(*following)
    for h, k in pairs:
        first(h, k).wait_send()
        second(h, k).wait_send()
        others(lambda peer: third(h, k, peer, z).wait_send())
        others(lambda peer: fourth(h, k, peer, z).wait_send())
        fifth(h, k, my_quarter(h, k)).wait_send()
        sixth(h, k, my_half(h, k)).wait_send()


def solution(mesh):
    n_wide, n_narrow = mesh.shape["wide"], mesh.shape["narrow"]

    def body(passages, centroids):
        m, d = passages.shape
        n = centroids.shape[0]
        reduce_here = n_wide % 4 == 0 and n % (8 * 2 * CHUNKS * n_wide) == 0
        dma = pltpu.SemaphoreType.DMA
        scratch = [
            pltpu.VMEM((m, n), jnp.float32),
            pltpu.VMEM((m, LANES), jnp.float32),
            pltpu.VMEM((1, n), jnp.float32),
            pltpu.VMEM((1, n), jnp.float32),
            pltpu.VMEM((1, m), jnp.float32),
            pltpu.VMEM((SWEEPS, n_narrow, 1, m), jnp.float32),
            pltpu.VMEM((SWEEPS, n_wide, 1, n), jnp.float32),
            dma((SWEEPS, n_narrow)),
            dma((SWEEPS, n_narrow)),
            dma((SWEEPS, n_wide)),
            dma((SWEEPS, n_wide)),
        ]
        if reduce_here:
            r = n // 2 // CHUNKS
            line = n_wide // 4
            scratch += [
                pltpu.VMEM((n, d), jnp.float32),
                pltpu.VMEM((2, CHUNKS, r // 2, d), jnp.float32),
                pltpu.VMEM((2, CHUNKS, r // 4, d), jnp.float32),
                pltpu.VMEM((2, CHUNKS, line, r // 4 // line, d), jnp.float32),
            ]
            pair, lines = dma((2, CHUNKS)), dma((2, CHUNKS, line))
            scratch += [pair] * 4 + [lines] * 4 + [pair] * 4
        vmem = pl.BlockSpec(memory_space=pltpu.VMEM)
        totals, row_potential, col_potential = pl.pallas_call(
            functools.partial(kernel, n_wide, n_narrow, reduce_here),
            out_shape=(
                jax.ShapeDtypeStruct((n, d), jnp.float32),
                jax.ShapeDtypeStruct((1, m), jnp.float32),
                jax.ShapeDtypeStruct((1, n), jnp.float32),
            ),
            in_specs=[vmem, vmem],
            out_specs=(vmem, vmem, vmem),
            scratch_shapes=scratch,
            compiler_params=pltpu.CompilerParams(
                collective_id=0, has_side_effects=True, vmem_limit_bytes=VMEM_LIMIT
            ),
        )(passages, centroids)
        if not reduce_here:
            totals = unit_rows(lax.psum(totals, "wide"))
        return totals, row_potential.reshape(m), col_potential.reshape(n)

    in_specs = (P("wide", None), P("narrow", None))
    out_specs = (P("narrow", None), P("wide"), P("narrow"))
    return jax.shard_map(body, mesh=mesh, in_specs=in_specs, out_specs=out_specs, check_vma=False)
```

```python
import functools
import heapq

import jax
import jax.numpy as jnp
from jax import lax
from jax.experimental import pallas as pl
from jax.experimental.pallas import tpu as pltpu
from jax.sharding import PartitionSpec as P

VECTOR_DIMENSION = 768
CENTROIDS = 4096
SWEEPS = 3
LANES = 128
CHUNKS = 8
AHEAD = 2
VMEM_LIMIT = 38 * 1024 * 1024
MESH = pl.DeviceIdType.MESH

entropic_regularizer = 0.02
LOG2_E = 1.4426950408889634


def plan(chunks):
    pairs = [(half, chunk) for chunk in range(chunks) for half in range(2)]
    sizes = (0.5, 0.25, 0.25, 0.25, 0.25, 0.5)
    free = {"x": 0.0, "y": 0.0, "z": 0.0}
    events, order, issued = [], [], 0
    unit = 512.0 / chunks * 0.132

    def send(at, pair, stage):
        axes = ("x", "y") if pair[0] == 0 else ("y", "x")
        link = (axes[0], axes[1], "z", "z", axes[1], axes[0])[stage]
        free[link] = max(at, free[link]) + sizes[stage] * unit
        heapq.heappush(events, (free[link] + (3.4 if link == "z" else 1.8), len(order), pair, stage))

    clock = 0.0
    while issued < min(2 * AHEAD, len(pairs)):
        clock += 3.6 / chunks
        send(clock, pairs[issued], 0)
        issued += 1
    while events:
        at, _, pair, stage = heapq.heappop(events)
        clock = max(clock, at) + (2.8, 1.6, 1.2, 0.1, 0.1, 0.1)[stage] / chunks
        follows = stage == 0 and issued < len(pairs)
        order.append((pair, stage, pairs[issued] if follows else None))
        if stage < 5:
            send(clock, pair, stage + 1)
        if follows:
            clock += 3.6 / chunks
            send(clock, pairs[issued], 0)
            issued += 1
    return order


def unit_rows(totals):
    return totals * lax.rsqrt(jnp.mean(totals * totals, axis=1, keepdims=True) + 1e-06)


def lane_groups(values):
    total = values[:, :LANES]
    for start in range(LANES, values.shape[1], LANES):
        total = total + values[:, start : start + LANES]
    return total


def to_lanes(values):
    ones = jnp.ones((8, LANES), jnp.float32)
    sums = lax.dot_general(
        ones, values, (((1,), (1,)), ((), ())),
        precision=lax.Precision.HIGHEST, preferred_element_type=jnp.float32,
    )
    return sums[0:1, :]


def kernel(
    n_wide, n_narrow, reduce_here,
    p_ref, c_ref, out_ref, rowpot_ref, colpot_ref,
    k_ref, scale_ref, cent_ref, col_ref, row_ref,
    rows_ref, mass_ref, rows_send, rows_recv, mass_send, mass_recv, *reduce_refs,
):
    m, n = k_ref.shape
    wide, narrow = lax.axis_index("wide"), lax.axis_index("narrow")

    barrier = pltpu.get_barrier_semaphore()

    def greet_wide(step, carry):
        pl.semaphore_signal(
            barrier, inc=1, device_id={"wide": lax.rem(wide + step, n_wide)}, device_id_type=MESH
        )
        return carry

    def greet_narrow(step, carry):
        pl.semaphore_signal(
            barrier, inc=1, device_id={"narrow": lax.rem(narrow + step, n_narrow)}, device_id_type=MESH
        )
        return carry

    lax.fori_loop(1, n_wide, greet_wide, 0)
    lax.fori_loop(1, n_narrow, greet_narrow, 0)

    cb = 256
    for j in range(n // cb):
        values = c_ref[j * cb : (j + 1) * cb, :].astype(jnp.float32)
        squares = to_lanes(lane_groups(values * values))
        cent_ref[:, j * cb : (j + 1) * cb] = lax.rsqrt(
            squares * (1.0 / VECTOR_DIMENSION) + 1e-06
        ) * (LOG2_E / (VECTOR_DIMENSION * entropic_regularizer))

    bm, bn = 256, 512

    @pl.loop(0, m // bm)
    def _(i):
        at = pl.ds(pl.multiple_of(i * bm, bm), bm)
        block = p_ref[at, :]
        values = block.astype(jnp.float32)
        scale = lax.rsqrt(
            jnp.sum(lane_groups(values * values), axis=1, keepdims=True) * (1.0 / VECTOR_DIMENSION) + 1e-06
        )
        scale_ref[at, :] = jnp.broadcast_to(scale, (bm, LANES))
        total = jnp.zeros((bm, LANES), jnp.float32)
        for j in range(n // bn):
            cols = slice(j * bn, (j + 1) * bn)
            scores = lax.dot_general(
                block, c_ref[cols, :], (((1,), (1,)), ((), ())), preferred_element_type=jnp.float32
            )
            entries = jnp.exp2(scores * scale * cent_ref[:, cols])
            k_ref[at, cols] = entries
            total = total + lane_groups(entries)
        rows_ref[0, pl.ds(narrow, 1), :, at] = to_lanes(total)[None]

    pl.semaphore_wait(barrier, n_wide - 1 + n_narrow - 1)

    target = float(n_wide * m) / float(n_narrow * n)
    rb, wb = 128, 256

    def exchange(sweep, buffer, axis, me, size, send, recv):
        def copy(peer, slot):
            return pltpu.make_async_remote_copy(
                src_ref=buffer.at[sweep, slot],
                dst_ref=buffer.at[sweep, slot],
                send_sem=send.at[sweep, peer],
                recv_sem=recv.at[sweep, slot],
                device_id={axis: peer},
                device_id_type=MESH,
            )

        def start(step, carry):
            copy(lax.rem(me + step, size), me).start()
            return carry

        def arrive(step, carry):
            peer = lax.rem(me + step, size)
            copy(peer, peer).wait_recv()
            return carry

        def sent(step, carry):
            copy(lax.rem(me + step, size), me).wait_send()
            return carry

        lax.fori_loop(1, size, start, 0)
        lax.fori_loop(1, size, arrive, 0)
        lax.fori_loop(1, size, sent, 0)
        total = buffer[sweep, 0]
        for slot in range(1, size):
            total = total + buffer[sweep, slot]
        return total

    for sweep in range(SWEEPS):
        if sweep > 0:

            @pl.loop(0, m // wb)
            def _(i):
                at = pl.ds(pl.multiple_of(i * wb, wb), wb)
                total = jnp.zeros((wb, LANES), jnp.float32)
                for t in range(n // LANES):
                    cols = slice(t * LANES, (t + 1) * LANES)
                    total = total + k_ref[at, cols] * col_ref[:, cols]
                rows_ref[sweep, pl.ds(narrow, 1), :, at] = to_lanes(total)[None]

        row_factor = 1.0 / exchange(sweep, rows_ref, "narrow", narrow, n_narrow, rows_send, rows_recv)
        row_ref[...] = row_factor

        last = sweep == SWEEPS - 1

        def mass_step(i, partial):
            at = pl.ds(pl.multiple_of(i * rb, rb), rb)
            factor = jnp.transpose(jnp.broadcast_to(row_ref[:, at], (LANES, rb)))
            if last:
                scale_ref[at, :] = scale_ref[at, :] * factor
            sums = []
            for t in range(n // LANES):
                cols = slice(t * LANES, (t + 1) * LANES)
                product = k_ref[at, cols] * factor
                sums.append(partial[t] + jnp.sum(product.reshape(rb // 8, 8, LANES), axis=0))
            return tuple(sums)

        zeros = tuple(jnp.zeros((8, LANES), jnp.float32) for _ in range(n // LANES))
        sums = lax.fori_loop(0, m // rb, mass_step, zeros)
        for t in range(n // LANES):
            mass_ref[sweep, pl.ds(wide, 1), :, t * LANES : (t + 1) * LANES] = jnp.sum(
                sums[t], axis=0, keepdims=True
            )[None]
        if last:
            rowpot_ref[...] = jnp.log(CENTROIDS * row_factor)
        col_ref[...] = target / exchange(sweep, mass_ref, "wide", wide, n_wide, mass_send, mass_recv)

    colpot_ref[...] = jnp.log(col_ref[...])

    tb = 128

    def totals_block(into, start):
        cols = pl.ds(pl.multiple_of(start, tb), tb)
        weights = (k_ref[:, cols] * scale_ref[...] * col_ref[:, cols]).astype(jnp.bfloat16)
        into[cols, :] = lax.dot_general(
            weights, p_ref[...], (((0,), (0,)), ((), ())), preferred_element_type=jnp.float32
        )

    if not reduce_here:

        @pl.loop(0, n // tb)
        def _(j):
            totals_block(out_ref, j * tb)

        return

    t_ref, got1, got2, got3, s1, r1, s2, r2, s3, r3, s4, r4, s5, r5, s6, r6 = reduce_refs
    line = n_wide // 4
    half = n // 2
    r = half // CHUNKS
    z, y, x = wide // 4, lax.rem(wide // 2, 2), lax.rem(wide, 2)
    over_x = z * 4 + y * 2 + (1 - x)
    over_y = z * 4 + (1 - y) * 2 + x
    partners = ((over_x, over_y), (over_y, over_x))
    bits = ((x, y), (y, x))
    plane = lax.rem(wide, 4)

    def rows_of(start, size):
        return pl.ds(pl.multiple_of(start, 8), size)

    def remote(src, dst, send, recv, peer):
        return pltpu.make_async_remote_copy(
            src_ref=src, dst_ref=dst, send_sem=send, recv_sem=recv,
            device_id={"wide": peer}, device_id_type=MESH,
        )

    def base(h, k):
        return h * half + k * r

    def my_half(h, k):
        return base(h, k) + bits[h][0] * (r // 2)

    def other_half(h, k):
        return base(h, k) + (1 - bits[h][0]) * (r // 2)

    def my_quarter(h, k):
        return my_half(h, k) + bits[h][1] * (r // 4)

    def other_quarter(h, k):
        return my_half(h, k) + (1 - bits[h][1]) * (r // 4)

    shard = r // 4 // line

    def first(h, k):
        return remote(
            t_ref.at[rows_of(other_half(h, k), r // 2)], got1.at[h, k],
            s1.at[h, k], r1.at[h, k], partners[h][0],
        )

    def second(h, k):
        return remote(
            t_ref.at[rows_of(other_quarter(h, k), r // 4)], got2.at[h, k],
            s2.at[h, k], r2.at[h, k], partners[h][1],
        )

    def third(h, k, peer, slot):
        return remote(
            t_ref.at[rows_of(my_quarter(h, k) + peer * shard, shard)], got3.at[h, k, slot],
            s3.at[h, k, peer], r3.at[h, k, slot], peer * 4 + plane,
        )

    def fourth(h, k, peer, slot):
        piece = rows_of(my_quarter(h, k) + slot * shard, shard)
        return remote(
            out_ref.at[piece], out_ref.at[piece],
            s4.at[h, k, peer], r4.at[h, k, slot], peer * 4 + plane,
        )

    def fifth(h, k, start):
        piece = rows_of(start, r // 4)
        return remote(
            out_ref.at[piece], out_ref.at[piece], s5.at[h, k], r5.at[h, k], partners[h][1]
        )

    def sixth(h, k, start):
        piece = rows_of(start, r // 2)
        return remote(
            out_ref.at[piece], out_ref.at[piece], s6.at[h, k], r6.at[h, k], partners[h][0]
        )

    def others(action):
        for step in range(1, line):
            action(lax.rem(z + step, line))

    pairs = [(h, k) for k in range(CHUNKS) for h in range(2)]

    def begin(h, k):
        @pl.loop(0, r // tb)
        def _(j):
            totals_block(t_ref, base(h, k) + j * tb)

        first(h, k).start()

    def add_first(h, k, quarter):
        at = rows_of(quarter, r // 4)
        t_ref[at, :] = t_ref[at, :] + got1[h, k, rows_of(quarter - my_half(h, k), r // 4), :]

    def after_first(h, k):
        first(h, k).wait_recv()
        add_first(h, k, other_quarter(h, k))
        second(h, k).start()
        add_first(h, k, my_quarter(h, k))

    def after_second(h, k):
        second(h, k).wait_recv()
        at = rows_of(my_quarter(h, k), r // 4)
        t_ref[at, :] = t_ref[at, :] + got2[h, k]
        others(lambda peer: third(h, k, peer, z).start())

    def after_third(h, k):
        others(lambda peer: third(h, k, z, peer).wait_recv())
        at = rows_of(my_quarter(h, k) + z * shard, shard)
        total = t_ref[at, :]
        for step in range(1, line):
            total = total + got3[h, k, lax.rem(z + step, line)]
        out_ref[at, :] = unit_rows(total)
        others(lambda peer: fourth(h, k, peer, z).start())

    def after_fourth(h, k):
        others(lambda peer: fourth(h, k, z, peer).wait_recv())
        fifth(h, k, my_quarter(h, k)).start()

    def after_fifth(h, k):
        fifth(h, k, other_quarter(h, k)).wait_recv()
        sixth(h, k, my_half(h, k)).start()

    def after_sixth(h, k):
        sixth(h, k, other_half(h, k)).wait_recv()

    stages = (after_first, after_second, after_third, after_fourth, after_fifth, after_sixth)
    for pair in pairs[: 2 * AHEAD]:
        begin(*pair)
    for pair, stage, following in plan(CHUNKS):
        stages[stage](*pair)
        if following is not None:
            begin(*following)
    for h, k in pairs:
        first(h, k).wait_send()
        second(h, k).wait_send()
        others(lambda peer: third(h, k, peer, z).wait_send())
        others(lambda peer: fourth(h, k, peer, z).wait_send())
        fifth(h, k, my_quarter(h, k)).wait_send()
        sixth(h, k, my_half(h, k)).wait_send()


def solution(mesh):
    n_wide, n_narrow = mesh.shape["wide"], mesh.shape["narrow"]

    def body(passages, centroids):
        m, d = passages.shape
        n = centroids.shape[0]
        reduce_here = n_wide % 4 == 0 and n % (8 * 2 * CHUNKS * n_wide) == 0
        dma = pltpu.SemaphoreType.DMA
        scratch = [
            pltpu.VMEM((m, n), jnp.float32),
            pltpu.VMEM((m, LANES), jnp.float32),
            pltpu.VMEM((1, n), jnp.float32),
            pltpu.VMEM((1, n), jnp.float32),
            pltpu.VMEM((1, m), jnp.float32),
            pltpu.VMEM((SWEEPS, n_narrow, 1, m), jnp.float32),
            pltpu.VMEM((SWEEPS, n_wide, 1, n), jnp.float32),
            dma((SWEEPS, n_narrow)),
            dma((SWEEPS, n_narrow)),
            dma((SWEEPS, n_wide)),
            dma((SWEEPS, n_wide)),
        ]
        if reduce_here:
            r = n // 2 // CHUNKS
            line = n_wide // 4
            scratch += [
                pltpu.VMEM((n, d), jnp.float32),
                pltpu.VMEM((2, CHUNKS, r // 2, d), jnp.float32),
                pltpu.VMEM((2, CHUNKS, r // 4, d), jnp.float32),
                pltpu.VMEM((2, CHUNKS, line, r // 4 // line, d), jnp.float32),
            ]
            pair, lines = dma((2, CHUNKS)), dma((2, CHUNKS, line))
            scratch += [pair] * 4 + [lines] * 4 + [pair] * 4
        vmem = pl.BlockSpec(memory_space=pltpu.VMEM)
        totals, row_potential, col_potential = pl.pallas_call(
            functools.partial(kernel, n_wide, n_narrow, reduce_here),
            out_shape=(
                jax.ShapeDtypeStruct((n, d), jnp.float32),
                jax.ShapeDtypeStruct((1, m), jnp.float32),
                jax.ShapeDtypeStruct((1, n), jnp.float32),
            ),
            in_specs=[vmem, vmem],
            out_specs=(vmem, vmem, vmem),
            scratch_shapes=scratch,
            compiler_params=pltpu.CompilerParams(
                collective_id=0, has_side_effects=True, vmem_limit_bytes=VMEM_LIMIT
            ),
        )(passages, centroids)
        if not reduce_here:
            totals = unit_rows(lax.psum(totals, "wide"))
        return totals, row_potential.reshape(m), col_potential.reshape(n)

    in_specs = (P("wide", None), P("narrow", None))
    out_specs = (P("narrow", None), P("wide"), P("narrow"))
    return jax.shard_map(body, mesh=mesh, in_specs=in_specs, out_specs=out_specs, check_vma=False)
```
